32 devices in a mesh: row: 4 (over x, core), col: 8 (over z, y).
Axes of the slice: x: 2, y: 2, z: 4, core: 2. Of those that a mesh axis runs over, the one named last changes fastest.
Arguments:
- features: bfloat16 [16384, 512], P(('col', 'row')), may hold values from -6 to 6
- blocks: bfloat16 [4, 8, 48, 128, 128], P('row', 'col'), may hold values from -0.25 to 0.25
- positions: int32 [4, 8, 48], P('row', 'col'), may hold values from 0 to 511, as said below
- counts: int32 [4, 8], P('row', 'col'), may hold values from 8 to 48, as said below
- weight: bfloat16 [512, 512], replicated, may hold values from -0.25 to 0.25
- bias: float32 [512], replicated, may hold values from -3 to 3
- cotangent: bfloat16 [16384, 512], P(('row', 'col')), may hold values from -6 to 6
Outputs:
- activated: bfloat16 [16384, 512], P(('row', 'col'))
- grad_weight: float32 [512, 512], replicated
- grad_bias: float32 [512], replicated
- grad_in: bfloat16 [16384, 512], P(('col', 'row'))
The draws below stay inside these ranges and needn't reach their ends.
Inputs may be any that keep to these rules, and one draw needn't show every extreme that they name: `counts`: every tile uses between 8 and 24 slots, except exactly one tile, which uses all 48. The 48 positions of one tile are distinct; only the first counts[i, j] of them are used.
All inputs are finite; a program needn't handle non-finite values.
Results may differ from the reference program's by a relative error of at most 0.0069.
Values may be sent and summed in bfloat16 or wider, within the bound.
No kernel may reach another device: no remote copies, remote signals or barrier semaphores. Data moves between devices by JAX's collectives and lax.ppermute only.
A program may use at most 64 MiB of HBM per device.

```python
import jax
import jax.numpy as jnp
from jax import lax

F = 512
BLOCK = 128
TC = 16
TR = 32
SLOTS = 8
MAXB = 48
NODES = 16384
N_ROW = 4
N_COL = 8


def tile_layout(key):
    key_counts = jax.random.fold_in(key, 11)
    key_heavy = jax.random.fold_in(key, 12)
    key_perm = jax.random.fold_in(key, 13)
    tiles = N_ROW * N_COL
    base_counts = jax.random.randint(key_counts, (tiles,), SLOTS, 3 * SLOTS + 1, dtype=jnp.int32)
    heavy_tile = jax.random.randint(key_heavy, (), 0, tiles, dtype=jnp.int32)
    tile_counts = jnp.where(jnp.arange(tiles, dtype=jnp.int32) == heavy_tile, MAXB, base_counts)
    perm_keys = jax.random.split(key_perm, tiles)
    orders = jax.vmap(lambda one_key: jax.random.permutation(one_key, TR * TC))(perm_keys)
    slot_pos = orders[:, :MAXB].astype(jnp.int32)
    return (tile_counts.astype(jnp.int32).reshape(N_ROW, N_COL), slot_pos.reshape(N_ROW, N_COL, MAXB))


def draw_counts(key, part):
    return tile_layout(key)[0]


def draw_positions(key, part):
    return tile_layout(key)[1]


def level_of(rng, extent, pieces, low, largest):
    loudness, own = 1.0, jax.random.fold_in(rng, 6)
    for dim, parts in pieces:
        steps = jnp.exp(jax.random.uniform(jax.random.fold_in(own, dim), (parts,), jnp.float32, low / len(pieces), largest / len(pieces)))
        loudness = loudness * jnp.repeat(steps, extent[dim] // parts).reshape([-1 if axis == dim else 1 for axis in range(len(extent))])
    return loudness


def normal_values(stream_key, extent, scale, bound, shards=(), kind=jnp.bfloat16):
    values = jax.random.normal(stream_key, extent, jnp.float32) * scale
    if len(shards) > 0:
        values = level_of(stream_key, extent, shards, -0.22, 0.18) * values
    return jnp.clip(values, min=-bound, max=bound).astype(kind)


def setup_inputs(seed: int = 0) -> dict:
    key_of = jax.random.split(jax.random.key(seed), 8)
    return {
        "features": normal_values(key_of[0], (NODES, F), 1.0, 6.0, ((0, 32),)),
        "blocks": normal_values(key_of[1], (N_ROW, N_COL, MAXB, BLOCK, BLOCK), (N_COL * MAXB * BLOCK // (3 * TR)) ** -0.5, 0.25, ((0, 4), (1, 8))),
        "positions": draw_positions(jax.random.fold_in(key_of[7], 71), 0),
        "counts": draw_counts(jax.random.fold_in(key_of[7], 71), 0),
        "weight": normal_values(key_of[4], (F, F), F ** -0.5, 0.25),
        "bias": normal_values(key_of[5], (F,), 0.5, 3.0, (), jnp.float32),
        "cotangent": normal_values(key_of[6], (NODES, F), 1.0, 6.0, ((0, 32),)),
    }


def round_tile(local):
    return lax.optimization_barrier(local.astype(jnp.bfloat16)).astype(jnp.float32)


def forward_tile(i_index, j_index, tile_vals, slot_pos, limit, source_blocks):
    def one_group(group, carried):
        start = (group * SLOTS).astype(jnp.int32)
        block_vals = lax.dynamic_slice_in_dim(tile_vals, start, SLOTS, 0).astype(jnp.float32)
        picked_pos = lax.dynamic_slice_in_dim(slot_pos, start, SLOTS, 0).astype(jnp.int32)
        in_rows = (j_index * TC + picked_pos % TC).astype(jnp.int32)
        alive = ((start + jnp.arange(SLOTS, dtype=jnp.int32)) < limit).astype(jnp.float32)
        picked = source_blocks[in_rows].astype(jnp.float32)
        products = jnp.einsum('sab,sbf->saf', block_vals, picked)
        return carried.at[picked_pos // TC].add(products * alive[:, None, None])

    groups = ((limit + SLOTS - 1) // SLOTS).astype(jnp.int32)
    local = lax.fori_loop(jnp.int32(0), groups, one_group, jnp.zeros((TR, BLOCK, F), jnp.float32))
    return round_tile(local)


def backward_tile(i_index, j_index, tile_vals, slot_pos, limit, source_blocks):
    def one_group(group, carried):
        start = (group * SLOTS).astype(jnp.int32)
        block_vals = lax.dynamic_slice_in_dim(tile_vals, start, SLOTS, 0).astype(jnp.float32)
        picked_pos = lax.dynamic_slice_in_dim(slot_pos, start, SLOTS, 0).astype(jnp.int32)
        out_rows = (i_index * TR + picked_pos // TC).astype(jnp.int32)
        alive = ((start + jnp.arange(SLOTS, dtype=jnp.int32)) < limit).astype(jnp.float32)
        picked = source_blocks[out_rows].astype(jnp.float32)
        products = jnp.einsum('sab,saf->sbf', block_vals, picked)
        return carried.at[picked_pos % TC].add(products * alive[:, None, None])

    groups = ((limit + SLOTS - 1) // SLOTS).astype(jnp.int32)
    local = lax.fori_loop(jnp.int32(0), groups, one_group, jnp.zeros((TC, BLOCK, F), jnp.float32))
    return round_tile(local)


def forward_all(blocks, positions, counts, source):
    source_blocks = source.reshape(NODES // BLOCK, BLOCK, F)

    def one_row(item):
        i_index, row_vals, row_pos, row_counts = item

        def scan_body(totals, inner):
            j_index, tile_vals, slot_pos, limit = inner
            return totals + forward_tile(i_index, j_index, tile_vals, slot_pos, limit, source_blocks), None

        totals, _ = lax.scan(scan_body, jnp.zeros((TR, BLOCK, F), jnp.float32),
                             (jnp.arange(N_COL, dtype=jnp.int32), row_vals, row_pos.astype(jnp.int32),
                              row_counts.astype(jnp.int32)))
        return totals

    result = lax.map(one_row, (jnp.arange(N_ROW, dtype=jnp.int32), blocks, positions, counts))
    return result.reshape(NODES, F)


def backward_all(blocks, positions, counts, source):
    source_blocks = source.reshape(NODES // BLOCK, BLOCK, F)

    def one_column(item):
        j_index, col_vals, col_pos, col_counts = item

        def scan_body(totals, inner):
            i_index, tile_vals, slot_pos, limit = inner
            return totals + backward_tile(i_index, j_index, tile_vals, slot_pos, limit, source_blocks), None

        totals, _ = lax.scan(scan_body, jnp.zeros((TC, BLOCK, F), jnp.float32),
                             (jnp.arange(N_ROW, dtype=jnp.int32), col_vals, col_pos.astype(jnp.int32),
                              col_counts.astype(jnp.int32)))
        return totals

    result = lax.map(one_column, (jnp.arange(N_COL, dtype=jnp.int32), jnp.swapaxes(blocks, 0, 1),
                                  jnp.swapaxes(positions, 0, 1), jnp.swapaxes(counts, 0, 1)))
    return result.reshape(NODES, F)


def reference(features, blocks, positions, counts, weight, bias, cotangent):
    aggregated = forward_all(blocks, positions, counts, features).astype(jnp.bfloat16)
    pre = jnp.dot(aggregated, weight, preferred_element_type=jnp.float32) + bias
    sigma = jax.nn.sigmoid(pre)
    activated = (pre * sigma).astype(jnp.bfloat16)
    grad_pre = (cotangent.astype(jnp.float32) * sigma * (1.0 + pre * (1.0 - sigma))).astype(jnp.bfloat16)
    grad_weight = jnp.dot(aggregated.T, grad_pre, preferred_element_type=jnp.float32)
    grad_bias = jnp.sum(grad_pre.astype(jnp.float32), axis=0)
    grad_mid = jnp.dot(grad_pre, weight.T, preferred_element_type=jnp.float32).astype(jnp.bfloat16)
    grad_in = backward_all(blocks, positions, counts, grad_mid).astype(jnp.bfloat16)
    return activated, grad_weight, grad_bias, grad_in
```

```python
import functools

import jax
import jax.numpy as jnp
from jax import lax
from jax.experimental import pallas as pl
from jax.experimental.pallas import tpu as pltpu
from jax.sharding import PartitionSpec as P

CHUNKS = 2

F32 = jnp.float32
BF16 = jnp.bfloat16
VMEM = pl.BlockSpec(memory_space=pltpu.VMEM)
SMEM = pl.BlockSpec(memory_space=pltpu.SMEM)
ANY = pl.BlockSpec(memory_space=pl.ANY)
VMEM_LIMIT = 48 * 1024 * 1024


def swap(value, axis, mask):
    size = lax.axis_size(axis)
    return lax.ppermute(value, axis, [(k, k ^ mask) for k in range(size)])


def slot_loop(meta, pos_ref, blocks_ref, a_buf, a_sem, half, first, body):
    count = meta[0]
    slots = a_buf.shape[0]

    def fetch(lo, hi, k):
        return pltpu.make_async_copy(blocks_ref.at[pl.ds(lo, hi - lo)], a_buf.at[pl.ds(lo, hi - lo)], a_sem.at[k])

    fetch(0, half, 0).start()

    @pl.when(count > half)
    def _():
        fetch(half, slots, 1).start()

    first()
    fetch(0, half, 0).wait()

    @pl.loop(0, jnp.minimum(count, half))
    def _(s):
        body(s, pos_ref[s])

    @pl.when(count > half)
    def _():
        fetch(half, slots, 1).wait()

        @pl.loop(half, count)
        def _(s):
            body(s, pos_ref[s])


def forward_kernel(n_parts, n_groups, tile_cols, meta, pos_ref, blocks_ref, *refs):
    parts = refs[:n_parts]
    keep = refs[n_parts : n_parts + n_groups]
    send = refs[n_parts + n_groups : n_parts + 2 * n_groups]
    x_buf, a_buf, total, x_sem, a_sem = refs[n_parts + 2 * n_groups :]
    block = a_buf.shape[-1]
    per_part = x_buf.shape[1] // block
    per_share = keep[0].shape[0] // block
    row, col = meta[1], meta[2]
    copies = [pltpu.make_async_copy(parts[k], x_buf.at[k], x_sem.at[k]) for k in range(n_parts)]
    for copy in copies:
        copy.start()

    def first():
        total[...] = jnp.zeros_like(total)
        for copy in copies:
            copy.wait()

    def body(s, where):
        r = where // tile_cols
        c = where % tile_cols
        start = pl.multiple_of((c % per_part) * block, block)
        x = x_buf[(c // per_part) ^ row, pl.ds(start, block), :]
        total[r] += jnp.dot(a_buf[s], x, preferred_element_type=F32)

    slot_loop(meta, pos_ref, blocks_ref, a_buf, a_sem, a_buf.shape[0] // 2, first, body)
    for k in range(n_groups):
        share = ((col // 2) ^ k) * 2
        for b in range(per_share):
            rows = pl.ds(b * block, block)
            keep[k][rows, :] = total[(share + col % 2) * per_share + b].astype(BF16)
            send[k][rows, :] = total[(share + 1 - col % 2) * per_share + b].astype(BF16)


def backward_kernel(n_parts, n_out, tile_cols, meta, pos_ref, blocks_ref, *refs):
    parts = refs[:n_parts]
    outs = refs[n_parts : n_parts + n_out]
    g_buf, a_buf, total, g_sem, a_sem = refs[n_parts + n_out :]
    block = a_buf.shape[-1]
    per_part = g_buf.shape[1] // block
    per_out = outs[0].shape[0] // block
    row, col = meta[1], meta[2]
    copies = [pltpu.make_async_copy(parts[k], g_buf.at[k], g_sem.at[k]) for k in range(n_parts)]
    for copy in copies:
        copy.start()

    def first():
        total[...] = jnp.zeros_like(total)
        for copy in copies:
            copy.wait()

    def body(s, where):
        r = where // tile_cols
        c = where % tile_cols
        start = pl.multiple_of((r % per_part) * block, block)
        g = g_buf[(r // per_part) ^ col, pl.ds(start, block), :]
        total[c] += lax.dot_general(a_buf[s], g, (((0,), (0,)), ((), ())), preferred_element_type=F32)

    slot_loop(meta, pos_ref, blocks_ref, a_buf, a_sem, a_buf.shape[0] // 2, first, body)
    for k in range(n_out):
        for b in range(per_out):
            outs[k][pl.ds(b * block, block), :] = total[(row ^ k) * per_out + b].astype(BF16)


def dense_kernel(n_parts, chunks, *refs):
    parts = refs[: n_parts * chunks]
    w_ref, b_ref, ct_ref = refs[n_parts * chunks : n_parts * chunks + 3]
    outs = refs[n_parts * chunks + 3 :]
    act_ref, gp_ref, gb_ref = outs[:3]
    agg_refs = outs[3 : 3 + chunks]
    mid_refs = outs[3 + chunks :]
    rows = act_ref.shape[0]
    width = act_ref.shape[1]
    fc = width // chunks
    pre = jnp.broadcast_to(b_ref[...], (rows, width))
    for f in range(chunks):
        mine = parts[f * n_parts : (f + 1) * n_parts]
        summed = mine[0][...].astype(F32)
        for part in mine[1:]:
            summed += part[...].astype(F32)
        agg = summed.astype(BF16)
        agg_refs[f][...] = agg
        pre += jnp.dot(agg, w_ref[pl.ds(f * fc, fc), :], preferred_element_type=F32)
    sigma = jax.nn.sigmoid(pre)
    act_ref[...] = (pre * sigma).astype(BF16)
    grad_pre = (ct_ref[...].astype(F32) * sigma * (1.0 + pre * (1.0 - sigma))).astype(BF16)
    gp_ref[...] = grad_pre

    @pl.when(pl.program_id(0) == 0)
    def _():
        gb_ref[...] = jnp.zeros_like(gb_ref)

    gb_ref[...] += jnp.sum(grad_pre.astype(F32).reshape(rows // 8, 8, width), axis=0)
    for f in range(chunks):
        mid_refs[f][...] = lax.dot_general(
            grad_pre, w_ref[pl.ds(f * fc, fc), :], (((1,), (1,)), ((), ())), preferred_element_type=F32
        ).astype(BF16)


def weight_kernel(chunks, meta, gp_ref, gb_ref, *refs):
    agg_refs = refs[:chunks]
    keep_ref, send_ref, total = refs[chunks:]
    width = gp_ref.shape[1]
    fc = width // chunks
    for f in range(chunks):
        total[pl.ds(f * fc, fc), :] = lax.dot_general(
            agg_refs[f][...], gp_ref[...], (((0,), (0,)), ((), ())), preferred_element_type=F32
        )
    half = width // 2
    mine = pl.multiple_of((meta[1] % 2) * half, half)
    theirs = pl.multiple_of((1 - meta[1] % 2) * half, half)
    keep_ref[...] = total[pl.ds(mine, half), :]
    send_ref[pl.ds(0, half), :] = total[pl.ds(theirs, half), :]
    send_ref[pl.ds(half, 8), :] = gb_ref[...]


def tree_sum(terms):
    while len(terms) > 1:
        terms = [terms[k] + terms[k + 1] for k in range(0, len(terms), 2)]
    return terms[0]


def reduce_level(piece, extra, axis, shift, number, place):
    size = piece.shape[0] // number
    kept = None
    others = []
    extras = [extra]
    for k in range(number):
        part = lax.dynamic_slice_in_dim(piece, (place ^ k) * size, size, 0)
        if k == 0:
            kept = part
        else:
            got = swap(jnp.concatenate([part, extra], axis=0), axis, k << shift)
            others.append(got[:size])
            extras.append(got[size:])
    return sum(others, kept), tree_sum(extras)


def gather_level(piece, axis, shift, number, place):
    size = piece.shape[0]
    pieces = [piece] + [swap(piece, axis, k << shift) for k in range(1, number)]
    if number == 2:
        low = place == 0
        return jnp.concatenate([jnp.where(low, pieces[0], pieces[1]), jnp.where(low, pieces[1], pieces[0])], axis=0)
    full = jnp.zeros((size * number, piece.shape[1]), piece.dtype)
    for k in range(number):
        full = lax.dynamic_update_slice_in_dim(full, pieces[k], (place ^ k) * size, 0)
    return full


def on_device(features, blocks, positions, counts, weight, bias, cotangent):
    block = blocks.shape[-1]
    slots = blocks.shape[2]
    shard_rows, width = features.shape
    share_rows = cotangent.shape[0]
    cols, rows = lax.axis_size("col"), lax.axis_size("row")
    col, row = lax.axis_index("col"), lax.axis_index("row")
    tile_cols = shard_rows * rows // block
    tile_rows = share_rows * cols // block
    groups = cols // 2
    fc = width // CHUNKS
    tile_vals = blocks[0, 0]
    slot_pos = positions[0, 0]
    meta = jnp.stack([counts[0, 0], row.astype(jnp.int32), col.astype(jnp.int32), jnp.int32(0)])
    params = pltpu.CompilerParams(vmem_limit_bytes=VMEM_LIMIT)
    slot_flops = 2 * slots * block * block * fc // 2

    aggregated = []
    for f in range(CHUNKS):
        own = features[:, f * fc : (f + 1) * fc]
        parts = []
        for k in range(rows // 2):
            near = own if k == 0 else swap(own, "row", 2 * k)
            parts += [near, swap(near, "row", 1)]
        out = jax.ShapeDtypeStruct((share_rows, fc), BF16)
        results = pl.pallas_call(
            functools.partial(forward_kernel, rows, groups, tile_cols),
            out_shape=[out] * (2 * groups),
            in_specs=[SMEM, SMEM] + [ANY] * (1 + rows),
            out_specs=[VMEM] * (2 * groups),
            scratch_shapes=[
                pltpu.VMEM((rows, shard_rows, fc), BF16),
                pltpu.VMEM((slots, block, block), BF16),
                pltpu.VMEM((tile_rows, block, fc), F32),
                pltpu.SemaphoreType.DMA((rows,)),
                pltpu.SemaphoreType.DMA((2,)),
            ],
            compiler_params=params,
            cost_estimate=pl.CostEstimate(
                flops=slot_flops, bytes_accessed=2 * (tile_cols + tile_rows) * block * fc, transcendentals=0
            ),
            name="forward_tile",
        )(meta, slot_pos, tile_vals, *parts)
        keep, send = results[:groups], results[groups:]
        terms = [keep[0], None]
        for k in list(range(1, groups)) + [0]:
            got = swap(send[k], "col", 1)
            if k == 0:
                terms[1] = got
            else:
                both = (keep[k].astype(F32) + got.astype(F32)).astype(BF16)
                terms.append(swap(both, "col", 2 * k))
        aggregated.append(terms)

    n_parts = len(aggregated[0])
    step = min(128, share_rows)
    tile = pl.BlockSpec((step, width), lambda n: (n, 0))
    part_tile = pl.BlockSpec((step, fc), lambda n: (n, 0))
    whole = lambda shape: pl.BlockSpec(shape, lambda n: (0, 0))
    part_shape = jax.ShapeDtypeStruct((share_rows, fc), BF16)
    full_shape = jax.ShapeDtypeStruct((share_rows, width), BF16)
    dense = pl.pallas_call(
        functools.partial(dense_kernel, n_parts, CHUNKS),
        grid=(share_rows // step,),
        out_shape=[full_shape, full_shape, jax.ShapeDtypeStruct((8, width), F32)] + [part_shape] * (2 * CHUNKS),
        in_specs=[part_tile] * (n_parts * CHUNKS) + [whole((width, width)), whole((1, width)), tile],
        out_specs=[tile, tile, whole((8, width))] + [part_tile] * (2 * CHUNKS),
        compiler_params=params,
        cost_estimate=pl.CostEstimate(
            flops=4 * share_rows * width * width, bytes_accessed=12 * share_rows * width, transcendentals=share_rows * width
        ),
        name="dense",
    )(*[term for terms in aggregated for term in terms], weight, bias.reshape(1, width), cotangent)
    activated, grad_pre, bias_term = dense[:3]
    agg = dense[3 : 3 + CHUNKS]
    mids = dense[3 + CHUNKS :]

    keep_w, send_w = pl.pallas_call(
        functools.partial(weight_kernel, CHUNKS),
        out_shape=[
            jax.ShapeDtypeStruct((width // 2, width), F32),
            jax.ShapeDtypeStruct((width // 2 + 8, width), F32),
        ],
        in_specs=[SMEM] + [VMEM] * (2 + CHUNKS),
        out_specs=[VMEM] * 2,
        scratch_shapes=[pltpu.VMEM((width, width), F32)],
        compiler_params=params,
        cost_estimate=pl.CostEstimate(
            flops=2 * share_rows * width * width, bytes_accessed=6 * width * width, transcendentals=0
        ),
        name="weight_term",
    )(meta, grad_pre, bias_term, *agg)
    got = swap(send_w, "row", 1)
    piece, extra = keep_w + got[: width // 2], bias_term + got[width // 2 :]
    piece, extra = reduce_level(piece, extra, "row", 1, rows // 2, row // 2)
    piece, extra = reduce_level(piece, extra, "col", 0, 2, col % 2)
    piece, extra = reduce_level(piece, extra, "col", 1, groups, col // 2)
    grad_bias = jnp.sum(extra, axis=0)
    piece = gather_level(piece, "col", 1, groups, col // 2)
    piece = gather_level(piece, "col", 0, 2, col % 2)
    piece = gather_level(piece, "row", 1, rows // 2, row // 2)
    grad_weight = gather_level(piece, "row", 0, 2, row % 2)

    pieces = []
    for f in range(CHUNKS):
        near = [mids[f]] + [swap(mids[f], "col", 2 * k) for k in range(1, groups)]
        parts = [part for value in near for part in (value, swap(value, "col", 1))]
        outs = pl.pallas_call(
            functools.partial(backward_kernel, cols, rows, tile_cols),
            out_shape=[jax.ShapeDtypeStruct((shard_rows, fc), BF16)] * rows,
            in_specs=[SMEM, SMEM] + [ANY] * (1 + cols),
            out_specs=[VMEM] * rows,
            scratch_shapes=[
                pltpu.VMEM((cols, share_rows, fc), BF16),
                pltpu.VMEM((slots, block, block), BF16),
                pltpu.VMEM((tile_cols, block, fc), F32),
                pltpu.SemaphoreType.DMA((cols,)),
                pltpu.SemaphoreType.DMA((2,)),
            ],
            compiler_params=params,
            cost_estimate=pl.CostEstimate(
                flops=slot_flops, bytes_accessed=2 * (tile_cols + tile_rows) * block * fc, transcendentals=0
            ),
            name="backward_tile",
        )(meta, slot_pos, tile_vals, *parts)
        final = None
        for k in list(range(1, rows // 2)) + [0]:
            got = swap(outs[2 * k + 1], "row", 1)
            both = outs[2 * k].astype(F32) + got.astype(F32)
            term = both if k == 0 else swap(both.astype(BF16), "row", 2 * k).astype(F32)
            final = term if final is None else final + term
        pieces.append(final.astype(BF16))
    grad_in = jnp.concatenate(pieces, axis=1)
    return activated, grad_weight, grad_bias, grad_in


def solution(mesh):
    placed = (
        P(("col", "row"), None),
        P("row", "col", None, None, None),
        P("row", "col", None),
        P("row", "col"),
        P(),
        P(),
        P(("row", "col"), None),
    )
    return jax.shard_map(
        on_device,
        mesh=mesh,
        in_specs=placed,
        out_specs=(P(("row", "col"), None), P(), P(), P(("col", "row"), None)),
        check_vma=False,
    )
```

```python
import functools

import jax
import jax.numpy as jnp
from jax import lax
from jax.experimental import pallas as pl
from jax.experimental.pallas import tpu as pltpu
from jax.sharding import PartitionSpec as P

CHUNKS = 2
UNROLL = 4

F32 = jnp.float32
BF16 = jnp.bfloat16
VMEM = pl.BlockSpec(memory_space=pltpu.VMEM)
SMEM = pl.BlockSpec(memory_space=pltpu.SMEM)
ANY = pl.BlockSpec(memory_space=pl.ANY)
HBM = pl.BlockSpec(memory_space=pltpu.HBM)
SMALL_LIMIT = 8 * 1024 * 1024
VMEM_LIMIT = 16 * 1024 * 1024


def swap(value, axis, mask):
    size = lax.axis_size(axis)
    return lax.ppermute(value, axis, [(k, k ^ mask) for k in range(size)])


def slot_loop(meta, blocks_ref, a_buf, a_sem, first, body):
    count = meta[0]
    slots = a_buf.shape[0]
    half = slots // 2

    def fetch(lo, hi, k):
        return pltpu.make_async_copy(blocks_ref.at[pl.ds(lo, hi - lo)], a_buf.at[pl.ds(lo, hi - lo)], a_sem.at[k])

    fetch(0, half, 0).start()

    @pl.when(count > half)
    def _():
        fetch(half, slots, 1).start()

    first()
    fetch(0, half, 0).wait()

    def step(g):
        picked = []
        for u in range(UNROLL):
            s = g * UNROLL + u
            picked.append((jnp.where(s < count, a_buf[s], jnp.zeros_like(a_buf[s])), meta[4 + s]))
        body(picked)

    @pl.loop(0, (jnp.minimum(count, half) + UNROLL - 1) // UNROLL)
    def _(g):
        step(g)

    @pl.when(count > half)
    def _():
        fetch(half, slots, 1).wait()

        @pl.loop(half // UNROLL, (count + UNROLL - 1) // UNROLL)
        def _(g):
            step(g)


def forward_kernel(n_parts, zs, tile_cols, meta, blocks_ref, *refs):
    parts = refs[:n_parts]
    keep = refs[n_parts : n_parts + zs]
    send = refs[n_parts + zs : n_parts + 2 * zs]
    x_buf, a_buf, total, x_sem, a_sem = refs[n_parts + 2 * zs :]
    block = a_buf.shape[-1]
    per_part = x_buf.shape[1] // block
    per_share = keep[0].shape[0] // block
    row, col = meta[1], meta[2]
    copies = [pltpu.make_async_copy(parts[k], x_buf.at[k], x_sem.at[k]) for k in range(n_parts)]
    for copy in copies:
        copy.start()

    def first():
        total[...] = jnp.zeros_like(total)
        for copy in copies:
            copy.wait()

    def body(picked):
        products = []
        for a, where in picked:
            c = where % tile_cols
            start = pl.multiple_of((c % per_part) * block, block)
            x = x_buf[(c // per_part) ^ row, pl.ds(start, block), :]
            products.append(jnp.dot(a, x, preferred_element_type=F32))
        for (_, where), product in zip(picked, products):
            total[where // tile_cols] += product

    slot_loop(meta, blocks_ref, a_buf, a_sem, first, body)
    for k in range(zs):
        share = ((col // 2) ^ k) * 2
        for b in range(per_share):
            rows = pl.ds(b * block, block)
            keep[k][rows, :] = total[(share + col % 2) * per_share + b].astype(BF16)
            send[k][rows, :] = total[(share + 1 - col % 2) * per_share + b].astype(BF16)


def backward_kernel(n_parts, chunk, whole_parts, tile_cols, meta, blocks_ref, *refs):
    parts = refs[:n_parts]
    keep_ref, send_ref = refs[n_parts : n_parts + 2]
    g_buf, a_buf, total, g_sem, a_sem = refs[n_parts + 2 :]
    block = a_buf.shape[-1]
    fc = g_buf.shape[2]
    per_part = g_buf.shape[1] // block
    n_out, per_out = keep_ref.shape[0], keep_ref.shape[1] // block
    row, col = meta[1], meta[2]
    copies = []
    for k in range(n_parts):
        source = parts[k].at[:, pl.ds(chunk * fc, fc)] if whole_parts[k] else parts[k]
        copies.append(pltpu.make_async_copy(source, g_buf.at[k], g_sem.at[k]))
        copies[-1].start()

    def first():
        total[...] = jnp.zeros_like(total)
        for copy in copies:
            copy.wait()

    def body(picked):
        products = []
        for a, where in picked:
            r = where // tile_cols
            start = pl.multiple_of((r % per_part) * block, block)
            g = g_buf[(r // per_part) ^ col, pl.ds(start, block), :]
            products.append(lax.dot_general(a, g, (((0,), (0,)), ((), ())), preferred_element_type=F32))
        for (_, where), product in zip(picked, products):
            total[where % tile_cols] += product

    slot_loop(meta, blocks_ref, a_buf, a_sem, first, body)
    for k in range(n_out):
        for b in range(per_out):
            rows = pl.ds(b * block, block)
            keep_ref[k, rows, :] = total[(row ^ (2 * k)) * per_out + b].astype(BF16)
            send_ref[k, rows, :] = total[(row ^ (2 * k + 1)) * per_out + b].astype(BF16)


def dense_kernel(n_parts, chunks, *refs):
    parts = refs[: n_parts * chunks]
    w_ref, b_ref, ct_ref = refs[n_parts * chunks : n_parts * chunks + 3]
    outs = refs[n_parts * chunks + 3 :]
    act_ref, gp_ref, agg_ref, gb_ref, mid_ref = outs[:5]
    mid_refs = outs[5:]
    rows = act_ref.shape[0]
    width = act_ref.shape[1]
    fc = width // chunks
    pre = jnp.broadcast_to(b_ref[...], (rows, width))
    for f in range(chunks):
        mine = parts[f * n_parts : (f + 1) * n_parts]
        summed = mine[0][...].astype(F32)
        for part in mine[1:]:
            summed += part[...].astype(F32)
        agg = summed.astype(BF16)
        agg_ref[:, pl.ds(f * fc, fc)] = agg
        pre += jnp.dot(agg, w_ref[pl.ds(f * fc, fc), :], preferred_element_type=F32)
    sigma = jax.nn.sigmoid(pre)
    act_ref[...] = (pre * sigma).astype(BF16)
    grad_pre = (ct_ref[...].astype(F32) * sigma * (1.0 + pre * (1.0 - sigma))).astype(BF16)
    gp_ref[...] = grad_pre

    @pl.when(pl.program_id(0) == 0)
    def _():
        gb_ref[...] = jnp.zeros_like(gb_ref)

    gb_ref[...] += jnp.sum(grad_pre.astype(F32).reshape(rows // 8, 8, width), axis=0)
    for f in range(chunks):
        mid = lax.dot_general(
            grad_pre, w_ref[pl.ds(f * fc, fc), :], (((1,), (1,)), ((), ())), preferred_element_type=F32
        ).astype(BF16)
        mid_ref[:, pl.ds(f * fc, fc)] = mid
        mid_refs[f][...] = mid


def weight_kernel(meta, agg_ref, gp_ref, gb_ref, keep_ref, send_ref, total):
    width = gp_ref.shape[1]
    half = width // 2
    for f in range(2):
        total[pl.ds(f * half, half), :] = lax.dot_general(
            agg_ref[:, pl.ds(f * half, half)], gp_ref[...], (((0,), (0,)), ((), ())), preferred_element_type=F32
        )
    mine = pl.multiple_of((meta[1] % 2) * half, half)
    theirs = pl.multiple_of((1 - meta[1] % 2) * half, half)
    keep_ref[...] = total[pl.ds(mine, half), :]
    send_ref[pl.ds(0, half), :] = total[pl.ds(theirs, half), :]
    send_ref[pl.ds(half, 8), :] = gb_ref[...]


def bit_of(meta, place):
    which, shift = place
    return (meta[which] >> shift) & 1


def halve_kernel(place, meta, keep_ref, extra_ref, got_ref, *outs):
    rows = keep_ref.shape[0]
    packet_ref = outs[-1]
    total = keep_ref[...] + got_ref[pl.ds(0, rows), :].astype(F32)
    extra = extra_ref[...] + got_ref[pl.ds(rows, 8), :].astype(F32)
    if place is None:
        packet_ref[pl.ds(0, rows), :] = total.astype(packet_ref.dtype)
        packet_ref[pl.ds(rows, 8), :] = extra.astype(packet_ref.dtype)
        return
    half = rows // 2
    low = bit_of(meta, place) == 0
    outs[0][...] = jnp.where(low, total[:half], total[half:])
    packet_ref[pl.ds(0, half), :] = jnp.where(low, total[half:], total[:half]).astype(packet_ref.dtype)
    packet_ref[pl.ds(half, 8), :] = extra.astype(packet_ref.dtype)
    outs[1][...] = extra.astype(packet_ref.dtype).astype(F32)


def join_kernel(place, meta, piece_ref, got_ref, out_ref):
    rows = piece_ref.shape[0]
    low = bit_of(meta, place) == 0
    piece, got = piece_ref[...], got_ref[...]
    out_ref[pl.ds(0, rows), :] = jnp.where(low, piece, got).astype(out_ref.dtype)
    out_ref[pl.ds(rows, rows), :] = jnp.where(low, got, piece).astype(out_ref.dtype)


def small_call(body, outs, *args):
    return pl.pallas_call(
        body,
        out_shape=outs,
        in_specs=[SMEM] + [VMEM] * (len(args) - 1),
        out_specs=[VMEM] * len(outs),
        compiler_params=pltpu.CompilerParams(vmem_limit_bytes=SMALL_LIMIT),
        cost_estimate=pl.CostEstimate(
            flops=0, bytes_accessed=sum(a.size * a.dtype.itemsize for a in args), transcendentals=0
        ),
    )(*args)


def halve(meta, keep, extra, got, place, kind):
    half, width = keep.shape[0] // 2, keep.shape[1]
    outs = [
        jax.ShapeDtypeStruct((half, width), F32),
        jax.ShapeDtypeStruct((8, width), F32),
        jax.ShapeDtypeStruct((half + 8, width), kind),
    ]
    return small_call(functools.partial(halve_kernel, place), outs, meta, keep, extra, got)


def double(meta, piece, axis, mask, place, kind):
    got = swap(piece, axis, mask)
    outs = [jax.ShapeDtypeStruct((2 * piece.shape[0], piece.shape[1]), kind)]
    return small_call(functools.partial(join_kernel, place), outs, meta, piece, got)[0]


def in_hbm(value):
    return pltpu.with_memory_space_constraint(value, pltpu.HBM)


def bits_below(number):
    return [1 << n for n in range(number.bit_length() - 1)]


def on_device(features, blocks, positions, counts, weight, bias, cotangent):
    block = blocks.shape[-1]
    slots = blocks.shape[2]
    shard_rows, width = features.shape
    share_rows = cotangent.shape[0]
    cols, rows = lax.axis_size("col"), lax.axis_size("row")
    col, row = lax.axis_index("col").astype(jnp.int32), lax.axis_index("row").astype(jnp.int32)
    tile_cols = shard_rows * rows // block
    tile_rows = share_rows * cols // block
    zs, xs = cols // 2, rows // 2
    fc = width // CHUNKS
    tile_vals = in_hbm(blocks[0, 0])
    meta = jnp.concatenate([jnp.stack([counts[0, 0], row, col, jnp.int32(0)]), positions[0, 0]])
    params = pltpu.CompilerParams(vmem_limit_bytes=VMEM_LIMIT)
    slot_cost = pl.CostEstimate(
        flops=slots * block * block * fc,
        bytes_accessed=2 * (tile_cols + tile_rows) * block * fc,
        transcendentals=0,
    )

    inputs = []
    for f in range(CHUNKS):
        own = features[:, f * fc : (f + 1) * fc]
        parts = []
        for k in range(xs):
            near = own if k == 0 else swap(own, "row", 2 * k)
            parts += [near, swap(near, "row", 1)]
        inputs.append(parts)
    aggregated = []
    for f in range(CHUNKS):
        out = jax.ShapeDtypeStruct((share_rows, fc), BF16)
        results = pl.pallas_call(
            functools.partial(forward_kernel, rows, zs, tile_cols),
            out_shape=[out] * (2 * zs),
            in_specs=[SMEM, HBM] + [ANY] * rows,
            out_specs=[VMEM] * (2 * zs),
            scratch_shapes=[
                pltpu.VMEM((rows, shard_rows, fc), BF16),
                pltpu.VMEM((slots, block, block), BF16),
                pltpu.VMEM((tile_rows, block, fc), F32),
                pltpu.SemaphoreType.DMA((rows,)),
                pltpu.SemaphoreType.DMA((2,)),
            ],
            compiler_params=params,
            cost_estimate=slot_cost,
            name="forward_tile",
        )(meta, tile_vals, *inputs[f])
        keep, send = results[:zs], results[zs:]
        arrived = [keep[0], swap(send[0], "col", 1)]
        for k in range(1, zs):
            got = swap(send[k], "col", 1)
            both = (keep[k].astype(F32) + got.astype(F32)).astype(BF16)
            arrived.append(swap(both, "col", 2 * k))
        aggregated.append(arrived)

    n_parts = len(aggregated[0])
    step = min(128, share_rows)
    tile = pl.BlockSpec((step, width), lambda n: (n, 0))
    part_tile = pl.BlockSpec((step, fc), lambda n: (n, 0))
    whole = lambda shape: pl.BlockSpec(shape, lambda n: (0, 0))
    part_shape = jax.ShapeDtypeStruct((share_rows, fc), BF16)
    full_shape = jax.ShapeDtypeStruct((share_rows, width), BF16)
    terms = [term for one in aggregated for term in one]
    dense = pl.pallas_call(
        functools.partial(dense_kernel, n_parts, CHUNKS),
        grid=(share_rows // step,),
        out_shape=[full_shape] * 3 + [jax.ShapeDtypeStruct((8, width), F32), full_shape] + [part_shape] * CHUNKS,
        in_specs=[part_tile] * len(terms) + [whole((width, width)), whole((1, width)), tile],
        out_specs=[tile] * 3 + [whole((8, width)), tile] + [part_tile] * CHUNKS,
        compiler_params=params,
        cost_estimate=pl.CostEstimate(
            flops=4 * share_rows * width * width, bytes_accessed=12 * share_rows * width, transcendentals=share_rows * width
        ),
        name="dense",
    )(*terms, weight, bias.reshape(1, width), cotangent)
    activated, grad_pre, agg, bias_term, mid = dense[:5]
    mids = dense[5:]

    near = [[swap(mids[f], "col", 2 * k) for k in range(1, zs)] for f in range(CHUNKS)]
    own_mirror = swap(mid, "col", 1)

    keep_w, send_w = pl.pallas_call(
        weight_kernel,
        out_shape=[jax.ShapeDtypeStruct((width // 2, width), F32), jax.ShapeDtypeStruct((width // 2 + 8, width), F32)],
        in_specs=[SMEM] + [VMEM] * 3,
        out_specs=[VMEM] * 2,
        scratch_shapes=[pltpu.VMEM((width, width), F32)],
        compiler_params=params,
        cost_estimate=pl.CostEstimate(
            flops=2 * share_rows * width * width, bytes_accessed=6 * width * width, transcendentals=0
        ),
        name="weight_term",
    )(meta, agg, grad_pre, bias_term)
    keep, extra, packet = keep_w, bias_term, send_w
    levels = [("wc", "row", 1, (1, 0))]
    levels += [(f"wx_{bit}", "row", 2 * bit, (1, bit.bit_length())) for bit in bits_below(xs)]
    levels += [("wy", "col", 1, (2, 0))]
    for n, (name, axis, mask, _) in enumerate(levels):
        got = swap(packet, axis, mask)
        if n + 1 < len(levels):
            kind = BF16 if n + 2 == len(levels) else F32
            keep, extra, packet = halve(meta, keep, extra, got, levels[n + 1][3], kind)
    left = keep.shape[0]
    (both,) = small_call(
        functools.partial(halve_kernel, None), [jax.ShapeDtypeStruct((left + 8, width), BF16)], meta, keep, extra, got
    )
    for bit in reversed(bits_below(zs)):
        both = (both.astype(F32) + swap(both, "col", 2 * bit).astype(F32)).astype(BF16)
    grad_bias = jnp.sum(both[left:].astype(F32), axis=0)
    piece = both[:left]
    for name, axis, mask, place in reversed(levels):
        piece = double(meta, piece, axis, mask, place, F32 if name == "wc" else BF16)
    grad_weight = piece

    for f in range(CHUNKS):
        parts = [mid, own_mirror]
        for k in range(1, zs):
            parts += [near[f][k - 1], swap(near[f][k - 1], "col", 1)]
        whole_parts = [True, True] + [False] * (cols - 2)
        keep_b, send_b = pl.pallas_call(
            functools.partial(backward_kernel, cols, f, tuple(whole_parts), tile_cols),
            out_shape=[jax.ShapeDtypeStruct((xs, shard_rows, fc), BF16)] * 2,
            in_specs=[SMEM, HBM] + [ANY] * cols,
            out_specs=[VMEM] * 2,
            scratch_shapes=[
                pltpu.VMEM((cols, share_rows, fc), BF16),
                pltpu.VMEM((slots, block, block), BF16),
                pltpu.VMEM((tile_cols, block, fc), F32),
                pltpu.SemaphoreType.DMA((cols,)),
                pltpu.SemaphoreType.DMA((2,)),
            ],
            compiler_params=params,
            cost_estimate=slot_cost,
            name="backward_tile",
        )(meta, tile_vals, *parts)
        got = swap(send_b, "row", 1)
        final = [keep_b[0], got[0]]
        for k in range(1, xs):
            both = (keep_b[k].astype(F32) + got[k].astype(F32)).astype(BF16)
            final.append(swap(both, "row", 2 * k))
        final = sum(term.astype(F32) for term in final).astype(BF16)
        if f == 0:
            grad_in = jnp.concatenate([final] * CHUNKS, axis=1)
        else:
            grad_in = lax.dynamic_update_slice(lax.optimization_barrier(grad_in), final, (0, f * fc))
    return activated, grad_weight, grad_bias, grad_in


def solution(mesh):
    placed = (
        P(("col", "row"), None),
        P("row", "col", None, None, None),
        P("row", "col", None),
        P("row", "col"),
        P(),
        P(),
        P(("row", "col"), None),
    )

    return jax.shard_map(
        on_device,
        mesh=mesh,
        in_specs=placed,
        out_specs=(P(("row", "col"), None), P(), P(), P(("col", "row"), None)),
        check_vma=False,
    )
```

```python
import functools

import jax
import jax.numpy as jnp
from jax import lax
from jax.experimental import pallas as pl
from jax.experimental.pallas import tpu as pltpu
from jax.sharding import PartitionSpec as P

CHUNKS = 2
UNROLL = 12

F32 = jnp.float32
BF16 = jnp.bfloat16
VMEM = pl.BlockSpec(memory_space=pltpu.VMEM)
SMEM = pl.BlockSpec(memory_space=pltpu.SMEM)
ANY = pl.BlockSpec(memory_space=pl.ANY)
HBM = pl.BlockSpec(memory_space=pltpu.HBM)
SMALL_LIMIT = 8 * 1024 * 1024
VMEM_LIMIT = 16 * 1024 * 1024

INWARD = ((0, 1), (3, 2))
OUTWARD = ((1, 0), (2, 3))
INNER = ((1, 2), (2, 1))


def swap(value, axis, mask):
    size = lax.axis_size(axis)
    return lax.ppermute(value, axis, [(k, k ^ mask) for k in range(size)])


def hop(value, pairs):
    return lax.ppermute(value, "col", [(2 * a + y, 2 * b + y) for a, b in pairs for y in range(2)])


def rounded_sum(*terms):
    return sum(term.astype(F32) for term in terms).astype(BF16)


def scatter_terms(keep, got):
    number = len(keep)
    if number != 4:
        moved = [swap(rounded_sum(keep[k], got[k]), "col", 2 * k) for k in range(1, number)]
        return [keep[0], got[0]] + moved
    far = hop(rounded_sum(keep[3], got[3]), INWARD)
    middle = hop(rounded_sum(keep[2], got[2]), INWARD)
    passed = hop(rounded_sum(keep[2], got[2], far), INNER)
    inner = hop(rounded_sum(keep[3], got[3], middle), INNER)
    near = swap(rounded_sum(keep[1], got[1], passed), "col", 2)
    return [keep[0], got[0], inner, near]


def gather_pieces(mine, number):
    if number != 4:
        return [swap(mine, "col", 2 * k) for k in range(1, number)]
    near = swap(mine, "col", 2)
    inner = hop(mine, INNER)
    passed = hop(near, INNER)
    middle = passed + hop(inner, OUTWARD)
    far = inner + hop(passed, OUTWARD)
    return [near, middle, far]


def slot_loop(meta, blocks_ref, a_buf, a_sem, first, body):
    count = meta[0]
    slots = a_buf.shape[0]
    half = slots // 2

    def fetch(lo, hi, k):
        return pltpu.make_async_copy(blocks_ref.at[pl.ds(lo, hi - lo)], a_buf.at[pl.ds(lo, hi - lo)], a_sem.at[k])

    fetch(0, half, 0).start()

    @pl.when(count > half)
    def _():
        fetch(half, slots, 1).start()

    first()
    fetch(0, half, 0).wait()

    def step(g):
        picked = []
        for u in range(UNROLL):
            s = g * UNROLL + u
            picked.append((jnp.where(s < count, a_buf[s], jnp.zeros_like(a_buf[s])), meta[4 + s]))
        body(picked)

    @pl.loop(0, (jnp.minimum(count, half) + UNROLL - 1) // UNROLL)
    def _(g):
        step(g)

    @pl.when(count > half)
    def _():
        fetch(half, slots, 1).wait()

        @pl.loop(half // UNROLL, (count + UNROLL - 1) // UNROLL)
        def _(g):
            step(g)


def forward_kernel(n_parts, zs, tile_cols, meta, blocks_ref, *refs):
    parts = refs[:n_parts]
    keep = refs[n_parts : n_parts + zs]
    send = refs[n_parts + zs : n_parts + 2 * zs]
    x_buf, a_buf, total, x_sem, a_sem = refs[n_parts + 2 * zs :]
    block = a_buf.shape[-1]
    per_part = x_buf.shape[1] // block
    per_share = keep[0].shape[0] // block
    row, col = meta[1], meta[2]
    copies = [pltpu.make_async_copy(parts[k], x_buf.at[k], x_sem.at[k]) for k in range(n_parts)]
    for copy in copies:
        copy.start()

    def first():
        total[...] = jnp.zeros_like(total)
        for copy in copies:
            copy.wait()

    def body(picked):
        products = []
        for a, where in picked:
            c = where % tile_cols
            start = pl.multiple_of((c % per_part) * block, block)
            x = x_buf[(c // per_part) ^ row, pl.ds(start, block), :]
            products.append(jnp.dot(a, x, preferred_element_type=F32))
        for (_, where), product in zip(picked, products):
            total[where // tile_cols] += product

    slot_loop(meta, blocks_ref, a_buf, a_sem, first, body)
    for k in range(zs):
        share = ((col // 2) ^ k) * 2
        for b in range(per_share):
            rows = pl.ds(b * block, block)
            keep[k][rows, :] = total[(share + col % 2) * per_share + b].astype(BF16)
            send[k][rows, :] = total[(share + 1 - col % 2) * per_share + b].astype(BF16)


def backward_kernel(n_parts, chunk, whole_parts, tile_cols, meta, blocks_ref, *refs):
    parts = refs[:n_parts]
    keep_ref, send_ref = refs[n_parts : n_parts + 2]
    g_buf, a_buf, total, g_sem, a_sem = refs[n_parts + 2 :]
    block = a_buf.shape[-1]
    fc = g_buf.shape[2]
    per_part = g_buf.shape[1] // block
    n_out, per_out = keep_ref.shape[0], keep_ref.shape[1] // block
    row, col = meta[1], meta[2]
    copies = []
    for k in range(n_parts):
        source = parts[k].at[:, pl.ds(chunk * fc, fc)] if whole_parts[k] else parts[k]
        copies.append(pltpu.make_async_copy(source, g_buf.at[k], g_sem.at[k]))
        copies[-1].start()

    def first():
        total[...] = jnp.zeros_like(total)
        for copy in copies:
            copy.wait()

    def body(picked):
        products = []
        for a, where in picked:
            r = where // tile_cols
            start = pl.multiple_of((r % per_part) * block, block)
            g = g_buf[(r // per_part) ^ col, pl.ds(start, block), :]
            products.append(lax.dot_general(a, g, (((0,), (0,)), ((), ())), preferred_element_type=F32))
        for (_, where), product in zip(picked, products):
            total[where % tile_cols] += product

    slot_loop(meta, blocks_ref, a_buf, a_sem, first, body)
    for k in range(n_out):
        for b in range(per_out):
            rows = pl.ds(b * block, block)
            keep_ref[k, rows, :] = total[(row ^ (2 * k)) * per_out + b].astype(BF16)
            send_ref[k, rows, :] = total[(row ^ (2 * k + 1)) * per_out + b].astype(BF16)


def dense_kernel(n_parts, chunks, *refs):
    parts = refs[: n_parts * chunks]
    w_ref, b_ref, ct_ref = refs[n_parts * chunks : n_parts * chunks + 3]
    outs = refs[n_parts * chunks + 3 :]
    act_ref, gp_ref, agg_ref, gb_ref, mid_ref = outs[:5]
    mid_refs = outs[5:]
    rows = act_ref.shape[0]
    width = act_ref.shape[1]
    fc = width // chunks
    pre = jnp.broadcast_to(b_ref[...], (rows, width))
    for f in range(chunks):
        mine = parts[f * n_parts : (f + 1) * n_parts]
        summed = mine[0][...].astype(F32)
        for part in mine[1:]:
            summed += part[...].astype(F32)
        agg = summed.astype(BF16)
        agg_ref[:, pl.ds(f * fc, fc)] = agg
        pre += jnp.dot(agg, w_ref[pl.ds(f * fc, fc), :], preferred_element_type=F32)
    sigma = jax.nn.sigmoid(pre)
    act_ref[...] = (pre * sigma).astype(BF16)
    grad_pre = (ct_ref[...].astype(F32) * sigma * (1.0 + pre * (1.0 - sigma))).astype(BF16)
    gp_ref[...] = grad_pre

    @pl.when(pl.program_id(0) == 0)
    def _():
        gb_ref[...] = jnp.zeros_like(gb_ref)

    gb_ref[...] += jnp.sum(grad_pre.astype(F32).reshape(rows // 8, 8, width), axis=0)
    for f in range(chunks):
        mid = lax.dot_general(
            grad_pre, w_ref[pl.ds(f * fc, fc), :], (((1,), (1,)), ((), ())), preferred_element_type=F32
        ).astype(BF16)
        mid_ref[:, pl.ds(f * fc, fc)] = mid
        mid_refs[f][...] = mid


def weight_kernel(meta, agg_ref, gp_ref, gb_ref, keep_ref, send_ref, total):
    width = gp_ref.shape[1]
    half = width // 2
    for f in range(2):
        total[pl.ds(f * half, half), :] = lax.dot_general(
            agg_ref[:, pl.ds(f * half, half)], gp_ref[...], (((0,), (0,)), ((), ())), preferred_element_type=F32
        )
    mine = pl.multiple_of((meta[1] % 2) * half, half)
    theirs = pl.multiple_of((1 - meta[1] % 2) * half, half)
    keep_ref[...] = total[pl.ds(mine, half), :]
    send_ref[pl.ds(0, half), :] = total[pl.ds(theirs, half), :]
    send_ref[pl.ds(half, 8), :] = gb_ref[...]


def bit_of(meta, place):
    which, shift = place
    return (meta[which] >> shift) & 1


def halve_kernel(place, meta, keep_ref, extra_ref, got_ref, *outs):
    rows = keep_ref.shape[0]
    packet_ref = outs[-1]
    total = keep_ref[...] + got_ref[pl.ds(0, rows), :].astype(F32)
    extra = extra_ref[...] + got_ref[pl.ds(rows, 8), :].astype(F32)
    if place is None:
        packet_ref[pl.ds(0, rows), :] = total.astype(packet_ref.dtype)
        packet_ref[pl.ds(rows, 8), :] = extra.astype(packet_ref.dtype)
        return
    half = rows // 2
    low = bit_of(meta, place) == 0
    outs[0][...] = jnp.where(low, total[:half], total[half:])
    packet_ref[pl.ds(0, half), :] = jnp.where(low, total[half:], total[:half]).astype(packet_ref.dtype)
    packet_ref[pl.ds(half, 8), :] = extra.astype(packet_ref.dtype)
    outs[1][...] = extra.astype(packet_ref.dtype).astype(F32)


def join_kernel(place, meta, piece_ref, got_ref, out_ref):
    rows = piece_ref.shape[0]
    low = bit_of(meta, place) == 0
    piece, got = piece_ref[...], got_ref[...]
    out_ref[pl.ds(0, rows), :] = jnp.where(low, piece, got).astype(out_ref.dtype)
    out_ref[pl.ds(rows, rows), :] = jnp.where(low, got, piece).astype(out_ref.dtype)


def small_call(body, outs, *args):
    return pl.pallas_call(
        body,
        out_shape=outs,
        in_specs=[SMEM] + [VMEM] * (len(args) - 1),
        out_specs=[VMEM] * len(outs),
        compiler_params=pltpu.CompilerParams(vmem_limit_bytes=SMALL_LIMIT),
        cost_estimate=pl.CostEstimate(
            flops=0, bytes_accessed=sum(a.size * a.dtype.itemsize for a in args), transcendentals=0
        ),
    )(*args)


def halve(meta, keep, extra, got, place, kind):
    half, width = keep.shape[0] // 2, keep.shape[1]
    outs = [
        jax.ShapeDtypeStruct((half, width), F32),
        jax.ShapeDtypeStruct((8, width), F32),
        jax.ShapeDtypeStruct((half + 8, width), kind),
    ]
    return small_call(functools.partial(halve_kernel, place), outs, meta, keep, extra, got)


def double(meta, piece, axis, mask, place, kind):
    got = swap(piece, axis, mask)
    outs = [jax.ShapeDtypeStruct((2 * piece.shape[0], piece.shape[1]), kind)]
    return small_call(functools.partial(join_kernel, place), outs, meta, piece, got)[0]


def in_hbm(value):
    return pltpu.with_memory_space_constraint(value, pltpu.HBM)


def bits_below(number):
    return [1 << n for n in range(number.bit_length() - 1)]


def on_device(features, blocks, positions, counts, weight, bias, cotangent):
    block = blocks.shape[-1]
    slots = blocks.shape[2]
    shard_rows, width = features.shape
    share_rows = cotangent.shape[0]
    cols, rows = lax.axis_size("col"), lax.axis_size("row")
    col, row = lax.axis_index("col").astype(jnp.int32), lax.axis_index("row").astype(jnp.int32)
    tile_cols = shard_rows * rows // block
    tile_rows = share_rows * cols // block
    zs, xs = cols // 2, rows // 2
    fc = width // CHUNKS
    tile_vals = in_hbm(blocks[0, 0])
    meta = jnp.concatenate([jnp.stack([counts[0, 0], row, col, jnp.int32(0)]), positions[0, 0]])
    params = pltpu.CompilerParams(vmem_limit_bytes=VMEM_LIMIT)
    slot_cost = pl.CostEstimate(
        flops=slots * block * block * fc,
        bytes_accessed=2 * (tile_cols + tile_rows) * block * fc,
        transcendentals=0,
    )

    inputs = []
    for f in range(CHUNKS):
        own = features[:, f * fc : (f + 1) * fc]
        parts = []
        for k in range(xs):
            near = own if k == 0 else swap(own, "row", 2 * k)
            parts += [near, swap(near, "row", 1)]
        inputs.append(parts)
    aggregated = []
    for f in range(CHUNKS):
        out = jax.ShapeDtypeStruct((share_rows, fc), BF16)
        results = pl.pallas_call(
            functools.partial(forward_kernel, rows, zs, tile_cols),
            out_shape=[out] * (2 * zs),
            in_specs=[SMEM, HBM] + [ANY] * rows,
            out_specs=[VMEM] * (2 * zs),
            scratch_shapes=[
                pltpu.VMEM((rows, shard_rows, fc), BF16),
                pltpu.VMEM((slots, block, block), BF16),
                pltpu.VMEM((tile_rows, block, fc), F32),
                pltpu.SemaphoreType.DMA((rows,)),
                pltpu.SemaphoreType.DMA((2,)),
            ],
            compiler_params=params,
            cost_estimate=slot_cost,
            name="forward_tile",
        )(meta, tile_vals, *inputs[f])
        keep, send = results[:zs], results[zs:]
        got = [swap(send[k], "col", 1) for k in range(zs)]
        aggregated.append(scatter_terms(keep, got))

    n_parts = len(aggregated[0])
    step = min(128, share_rows)
    tile = pl.BlockSpec((step, width), lambda n: (n, 0))
    part_tile = pl.BlockSpec((step, fc), lambda n: (n, 0))
    whole = lambda shape: pl.BlockSpec(shape, lambda n: (0, 0))
    part_shape = jax.ShapeDtypeStruct((share_rows, fc), BF16)
    full_shape = jax.ShapeDtypeStruct((share_rows, width), BF16)
    terms = [term for one in aggregated for term in one]
    dense = pl.pallas_call(
        functools.partial(dense_kernel, n_parts, CHUNKS),
        grid=(share_rows // step,),
        out_shape=[full_shape] * 3 + [jax.ShapeDtypeStruct((8, width), F32), full_shape] + [part_shape] * CHUNKS,
        in_specs=[part_tile] * len(terms) + [whole((width, width)), whole((1, width)), tile],
        out_specs=[tile] * 3 + [whole((8, width)), tile] + [part_tile] * CHUNKS,
        compiler_params=params,
        cost_estimate=pl.CostEstimate(
            flops=4 * share_rows * width * width, bytes_accessed=12 * share_rows * width, transcendentals=share_rows * width
        ),
        name="dense",
    )(*terms, weight, bias.reshape(1, width), cotangent)
    activated, grad_pre, agg, bias_term, mid = dense[:5]
    mids = dense[5:]

    near = [gather_pieces(mids[f], zs) for f in range(CHUNKS)]
    own_mirror = swap(mid, "col", 1)

    keep_w, send_w = pl.pallas_call(
        weight_kernel,
        out_shape=[jax.ShapeDtypeStruct((width // 2, width), F32), jax.ShapeDtypeStruct((width // 2 + 8, width), F32)],
        in_specs=[SMEM] + [VMEM] * 3,
        out_specs=[VMEM] * 2,
        scratch_shapes=[pltpu.VMEM((width, width), F32)],
        compiler_params=params,
        cost_estimate=pl.CostEstimate(
            flops=2 * share_rows * width * width, bytes_accessed=6 * width * width, transcendentals=0
        ),
        name="weight_term",
    )(meta, agg, grad_pre, bias_term)
    keep, extra, packet = keep_w, bias_term, send_w
    levels = [("wc", "row", 1, (1, 0))]
    levels += [(f"wx_{bit}", "row", 2 * bit, (1, bit.bit_length())) for bit in bits_below(xs)]
    levels += [("wy", "col", 1, (2, 0))]
    for n, (name, axis, mask, _) in enumerate(levels):
        got = swap(packet, axis, mask)
        if n + 1 < len(levels):
            kind = BF16 if n + 2 == len(levels) else F32
            keep, extra, packet = halve(meta, keep, extra, got, levels[n + 1][3], kind)
    left = keep.shape[0]
    (both,) = small_call(
        functools.partial(halve_kernel, None), [jax.ShapeDtypeStruct((left + 8, width), BF16)], meta, keep, extra, got
    )
    for bit in reversed(bits_below(zs)):
        both = (both.astype(F32) + swap(both, "col", 2 * bit).astype(F32)).astype(BF16)
    grad_bias = jnp.sum(both[left:].astype(F32), axis=0)
    piece = both[:left]
    for name, axis, mask, place in reversed(levels):
        piece = double(meta, piece, axis, mask, place, F32 if name == "wc" else BF16)
    grad_weight = piece

    for f in range(CHUNKS):
        parts = [mid, own_mirror]
        for k in range(1, zs):
            parts += [near[f][k - 1], swap(near[f][k - 1], "col", 1)]
        whole_parts = [True, True] + [False] * (cols - 2)
        keep_b, send_b = pl.pallas_call(
            functools.partial(backward_kernel, cols, f, tuple(whole_parts), tile_cols),
            out_shape=[jax.ShapeDtypeStruct((xs, shard_rows, fc), BF16)] * 2,
            in_specs=[SMEM, HBM] + [ANY] * cols,
            out_specs=[VMEM] * 2,
            scratch_shapes=[
                pltpu.VMEM((cols, share_rows, fc), BF16),
                pltpu.VMEM((slots, block, block), BF16),
                pltpu.VMEM((tile_cols, block, fc), F32),
                pltpu.SemaphoreType.DMA((cols,)),
                pltpu.SemaphoreType.DMA((2,)),
            ],
            compiler_params=params,
            cost_estimate=slot_cost,
            name="backward_tile",
        )(meta, tile_vals, *parts)
        got = swap(send_b, "row", 1)
        final = [keep_b[0], got[0]]
        for k in range(1, xs):
            both = (keep_b[k].astype(F32) + got[k].astype(F32)).astype(BF16)
            final.append(swap(both, "row", 2 * k))
        final = sum(term.astype(F32) for term in final).astype(BF16)
        if f == 0:
            grad_in = jnp.concatenate([final] * CHUNKS, axis=1)
        else:
            grad_in = lax.dynamic_update_slice(lax.optimization_barrier(grad_in), final, (0, f * fc))
    return activated, grad_weight, grad_bias, grad_in


def solution(mesh):
    placed = (
        P(("col", "row"), None),
        P("row", "col", None, None, None),
        P("row", "col", None),
        P("row", "col"),
        P(),
        P(),
        P(("row", "col"), None),
    )

    return jax.shard_map(
        on_device,
        mesh=mesh,
        in_specs=placed,
        out_specs=(P(("row", "col"), None), P(), P(), P(("col", "row"), None)),
        check_vma=False,
    )
```

```python
import functools

import jax
import jax.numpy as jnp
from jax import lax
from jax.experimental import pallas as pl
from jax.experimental.pallas import tpu as pltpu
from jax.sharding import PartitionSpec as P

CHUNKS = 2
UNROLL = 12
STEP = 512

F32 = jnp.float32
BF16 = jnp.bfloat16
VMEM = pl.BlockSpec(memory_space=pltpu.VMEM)
SMEM = pl.BlockSpec(memory_space=pltpu.SMEM)
ANY = pl.BlockSpec(memory_space=pl.ANY)
HBM = pl.BlockSpec(memory_space=pltpu.HBM)
SMALL_LIMIT = 8 * 1024 * 1024
VMEM_LIMIT = 16 * 1024 * 1024

INWARD = ((0, 1), (3, 2))
OUTWARD = ((1, 0), (2, 3))
INNER = ((1, 2), (2, 1))


def swap(value, axis, mask):
    size = lax.axis_size(axis)
    return lax.ppermute(value, axis, [(k, k ^ mask) for k in range(size)])


def hop(value, pairs):
    return lax.ppermute(value, "col", [(2 * a + y, 2 * b + y) for a, b in pairs for y in range(2)])


def rounded_sum(*terms):
    return sum(term.astype(F32) for term in terms).astype(BF16)


def scatter_terms(keep, got):
    number = len(keep)
    if number != 4:
        moved = [swap(rounded_sum(keep[k], got[k]), "col", 2 * k) for k in range(1, number)]
        return [keep[0], got[0]] + moved
    far = hop(rounded_sum(keep[3], got[3]), INWARD)
    middle = hop(rounded_sum(keep[2], got[2]), INWARD)
    own, other, far = lax.optimization_barrier((keep[2], got[2], far))
    passed = hop(rounded_sum(own, other, far), INNER)
    own, other, middle = lax.optimization_barrier((keep[3], got[3], middle))
    inner = hop(rounded_sum(own, other, middle), INNER)
    near = swap(rounded_sum(keep[1], got[1], passed), "col", 2)
    return [keep[0], got[0], inner, near]


def gather_pieces(mine, number):
    if number != 4:
        return [swap(mine, "col", 2 * k) for k in range(1, number)]
    near = swap(mine, "col", 2)
    inner = hop(mine, INNER)
    passed = hop(near, INNER)
    outer = hop(inner, OUTWARD)
    middle = passed + outer
    outer = hop(passed, OUTWARD)
    far = inner + outer
    return [near, middle, far]


def slot_loop(meta, blocks_ref, a_buf, a_sem, first, body):
    count = meta[0]
    slots = a_buf.shape[0]
    half = slots // 2

    def fetch(lo, hi, k):
        return pltpu.make_async_copy(blocks_ref.at[pl.ds(lo, hi - lo)], a_buf.at[pl.ds(lo, hi - lo)], a_sem.at[k])

    fetch(0, half, 0).start()

    @pl.when(count > half)
    def _():
        fetch(half, slots, 1).start()

    first()
    fetch(0, half, 0).wait()

    def step(g):
        picked = []
        for u in range(UNROLL):
            s = g * UNROLL + u
            picked.append((jnp.where(s < count, a_buf[s], jnp.zeros_like(a_buf[s])), meta[4 + s]))
        body(picked)

    @pl.loop(0, (jnp.minimum(count, half) + UNROLL - 1) // UNROLL)
    def _(g):
        step(g)

    @pl.when(count > half)
    def _():
        fetch(half, slots, 1).wait()

        @pl.loop(half // UNROLL, (count + UNROLL - 1) // UNROLL)
        def _(g):
            step(g)


def forward_kernel(n_parts, zs, tile_cols, meta, blocks_ref, *refs):
    parts = refs[:n_parts]
    keep = refs[n_parts : n_parts + zs]
    send = refs[n_parts + zs : n_parts + 2 * zs]
    x_buf, a_buf, total, x_sem, a_sem = refs[n_parts + 2 * zs :]
    block = a_buf.shape[-1]
    per_part = x_buf.shape[1] // block
    per_share = keep[0].shape[0] // block
    row, col = meta[1], meta[2]
    copies = [pltpu.make_async_copy(parts[k], x_buf.at[k], x_sem.at[k]) for k in range(n_parts)]
    for copy in copies:
        copy.start()

    def first():
        total[...] = jnp.zeros_like(total)
        for copy in copies:
            copy.wait()

    def body(picked):
        products = []
        for a, where in picked:
            c = where % tile_cols
            start = pl.multiple_of((c % per_part) * block, block)
            x = x_buf[(c // per_part) ^ row, pl.ds(start, block), :]
            products.append(jnp.dot(a, x, preferred_element_type=F32))
        for (_, where), product in zip(picked, products):
            total[where // tile_cols] += product

    slot_loop(meta, blocks_ref, a_buf, a_sem, first, body)
    for k in range(zs):
        share = ((col // 2) ^ k) * 2
        for b in range(per_share):
            rows = pl.ds(b * block, block)
            keep[k][rows, :] = total[(share + col % 2) * per_share + b].astype(BF16)
            send[k][rows, :] = total[(share + 1 - col % 2) * per_share + b].astype(BF16)


def backward_kernel(n_parts, chunk, whole_parts, tile_cols, meta, blocks_ref, *refs):
    parts = refs[:n_parts]
    keep_ref, send_ref = refs[n_parts : n_parts + 2]
    g_buf, a_buf, total, g_sem, a_sem = refs[n_parts + 2 :]
    block = a_buf.shape[-1]
    fc = g_buf.shape[2]
    per_part = g_buf.shape[1] // block
    n_out, per_out = keep_ref.shape[0], keep_ref.shape[1] // block
    row, col = meta[1], meta[2]
    copies = []
    for k in range(n_parts):
        source = parts[k].at[:, pl.ds(chunk * fc, fc)] if whole_parts[k] else parts[k]
        copies.append(pltpu.make_async_copy(source, g_buf.at[k], g_sem.at[k]))
        copies[-1].start()

    def first():
        total[...] = jnp.zeros_like(total)
        for copy in copies:
            copy.wait()

    def body(picked):
        products = []
        for a, where in picked:
            r = where // tile_cols
            start = pl.multiple_of((r % per_part) * block, block)
            g = g_buf[(r // per_part) ^ col, pl.ds(start, block), :]
            products.append(lax.dot_general(a, g, (((0,), (0,)), ((), ())), preferred_element_type=F32))
        for (_, where), product in zip(picked, products):
            total[where % tile_cols] += product

    slot_loop(meta, blocks_ref, a_buf, a_sem, first, body)
    for k in range(n_out):
        for b in range(per_out):
            rows = pl.ds(b * block, block)
            keep_ref[k, rows, :] = total[(row ^ (2 * k)) * per_out + b].astype(BF16)
            send_ref[k, rows, :] = total[(row ^ (2 * k + 1)) * per_out + b].astype(BF16)


def dense_kernel(n_parts, chunks, *refs):
    parts = refs[: n_parts * chunks]
    w_ref, b_ref, ct_ref = refs[n_parts * chunks : n_parts * chunks + 3]
    outs = refs[n_parts * chunks + 3 :]
    act_ref, gp_ref, agg_ref, gb_ref, mid_ref = outs[:5]
    mid_refs = outs[5:]
    rows = act_ref.shape[0]
    width = act_ref.shape[1]
    fc = width // chunks
    pre = jnp.broadcast_to(b_ref[...], (rows, width))
    for f in range(chunks):
        mine = parts[f * n_parts : (f + 1) * n_parts]
        summed = mine[0][...].astype(F32)
        for part in mine[1:]:
            summed += part[...].astype(F32)
        agg = summed.astype(BF16)
        agg_ref[:, pl.ds(f * fc, fc)] = agg
        pre += jnp.dot(agg, w_ref[pl.ds(f * fc, fc), :], preferred_element_type=F32)
    sigma = jax.nn.sigmoid(pre)
    act_ref[...] = (pre * sigma).astype(BF16)
    grad_pre = (ct_ref[...].astype(F32) * sigma * (1.0 + pre * (1.0 - sigma))).astype(BF16)
    gp_ref[...] = grad_pre

    @pl.when(pl.program_id(0) == 0)
    def _():
        gb_ref[...] = jnp.zeros_like(gb_ref)

    gb_ref[...] += jnp.sum(grad_pre.astype(F32).reshape(rows // 8, 8, width), axis=0)
    for f in range(chunks):
        mid = lax.dot_general(
            grad_pre, w_ref[pl.ds(f * fc, fc), :], (((1,), (1,)), ((), ())), preferred_element_type=F32
        ).astype(BF16)
        mid_ref[:, pl.ds(f * fc, fc)] = mid
        mid_refs[f][...] = mid


def weight_kernel(meta, agg_ref, gp_ref, gb_ref, keep_ref, send_ref, total):
    width = gp_ref.shape[1]
    half = width // 2
    for f in range(2):
        total[pl.ds(f * half, half), :] = lax.dot_general(
            agg_ref[:, pl.ds(f * half, half)], gp_ref[...], (((0,), (0,)), ((), ())), preferred_element_type=F32
        )
    mine = pl.multiple_of((meta[1] % 2) * half, half)
    theirs = pl.multiple_of((1 - meta[1] % 2) * half, half)
    keep_ref[...] = total[pl.ds(mine, half), :]
    send_ref[pl.ds(0, half), :] = total[pl.ds(theirs, half), :]
    send_ref[pl.ds(half, 8), :] = gb_ref[...]


def bit_of(meta, place):
    which, shift = place
    return (meta[which] >> shift) & 1


def halve_kernel(place, meta, keep_ref, extra_ref, got_ref, *outs):
    rows = keep_ref.shape[0]
    packet_ref = outs[-1]
    total = keep_ref[...] + got_ref[pl.ds(0, rows), :].astype(F32)
    extra = extra_ref[...] + got_ref[pl.ds(rows, 8), :].astype(F32)
    if place is None:
        packet_ref[pl.ds(0, rows), :] = total.astype(packet_ref.dtype)
        packet_ref[pl.ds(rows, 8), :] = extra.astype(packet_ref.dtype)
        return
    half = rows // 2
    low = bit_of(meta, place) == 0
    outs[0][...] = jnp.where(low, total[:half], total[half:])
    packet_ref[pl.ds(0, half), :] = jnp.where(low, total[half:], total[:half]).astype(packet_ref.dtype)
    packet_ref[pl.ds(half, 8), :] = extra.astype(packet_ref.dtype)
    outs[1][...] = extra.astype(packet_ref.dtype).astype(F32)


def join_kernel(place, meta, piece_ref, got_ref, out_ref):
    rows = piece_ref.shape[0]
    low = bit_of(meta, place) == 0
    piece, got = piece_ref[...], got_ref[...]
    out_ref[pl.ds(0, rows), :] = jnp.where(low, piece, got).astype(out_ref.dtype)
    out_ref[pl.ds(rows, rows), :] = jnp.where(low, got, piece).astype(out_ref.dtype)


def final_kernel(n_near, meta, early_ref, keep_ref, got_ref, *refs):
    out_ref = refs[-1]
    early = early_ref.shape[1]
    out_ref[:, pl.ds(0, early)] = early_ref[...]
    total = keep_ref[0].astype(F32) + got_ref[0].astype(F32)
    for ref in refs[:n_near]:
        total += ref[...].astype(F32)
    out_ref[:, pl.ds(early, total.shape[1])] = total.astype(out_ref.dtype)


def small_call(body, outs, *args):
    return pl.pallas_call(
        body,
        out_shape=outs,
        in_specs=[SMEM] + [VMEM] * (len(args) - 1),
        out_specs=[VMEM] * len(outs),
        compiler_params=pltpu.CompilerParams(vmem_limit_bytes=SMALL_LIMIT),
        cost_estimate=pl.CostEstimate(
            flops=0, bytes_accessed=sum(a.size * a.dtype.itemsize for a in args), transcendentals=0
        ),
    )(*args)


def halve(meta, keep, extra, got, place, kind):
    half, width = keep.shape[0] // 2, keep.shape[1]
    outs = [
        jax.ShapeDtypeStruct((half, width), F32),
        jax.ShapeDtypeStruct((8, width), F32),
        jax.ShapeDtypeStruct((half + 8, width), kind),
    ]
    return small_call(functools.partial(halve_kernel, place), outs, meta, keep, extra, got)


def double(meta, piece, axis, mask, place, kind):
    got = swap(piece, axis, mask)
    outs = [jax.ShapeDtypeStruct((2 * piece.shape[0], piece.shape[1]), kind)]
    return small_call(functools.partial(join_kernel, place), outs, meta, piece, got)[0]


def in_hbm(value):
    return pltpu.with_memory_space_constraint(value, pltpu.HBM)


def bits_below(number):
    return [1 << n for n in range(number.bit_length() - 1)]


def on_device(features, blocks, positions, counts, weight, bias, cotangent):
    block = blocks.shape[-1]
    slots = blocks.shape[2]
    shard_rows, width = features.shape
    share_rows = cotangent.shape[0]
    cols, rows = lax.axis_size("col"), lax.axis_size("row")
    col, row = lax.axis_index("col").astype(jnp.int32), lax.axis_index("row").astype(jnp.int32)
    tile_cols = shard_rows * rows // block
    tile_rows = share_rows * cols // block
    zs, xs = cols // 2, rows // 2
    fc = width // CHUNKS
    tile_vals = in_hbm(blocks[0, 0])
    meta = jnp.concatenate([jnp.stack([counts[0, 0], row, col, jnp.int32(0)]), positions[0, 0]])
    params = pltpu.CompilerParams(vmem_limit_bytes=VMEM_LIMIT)
    slot_cost = pl.CostEstimate(
        flops=slots * block * block * fc,
        bytes_accessed=2 * (tile_cols + tile_rows) * block * fc,
        transcendentals=0,
    )

    inputs = []
    for f in range(CHUNKS):
        source = features if f == 0 else lax.optimization_barrier(features)
        own = source[:, f * fc : (f + 1) * fc]
        parts = []
        for k in range(xs):
            near = own if k == 0 else swap(own, "row", 2 * k)
            parts += [near, swap(near, "row", 1)]
        inputs.append(parts)
    aggregated = []
    for f in range(CHUNKS):
        out = jax.ShapeDtypeStruct((share_rows, fc), BF16)
        results = pl.pallas_call(
            functools.partial(forward_kernel, rows, zs, tile_cols),
            out_shape=[out] * (2 * zs),
            in_specs=[SMEM, HBM] + [ANY] * rows,
            out_specs=[VMEM] * (2 * zs),
            scratch_shapes=[
                pltpu.VMEM((rows, shard_rows, fc), BF16),
                pltpu.VMEM((slots, block, block), BF16),
                pltpu.VMEM((tile_rows, block, fc), F32),
                pltpu.SemaphoreType.DMA((rows,)),
                pltpu.SemaphoreType.DMA((2,)),
            ],
            compiler_params=params,
            cost_estimate=slot_cost,
            name="fwd",
        )(meta, tile_vals, *inputs[f])
        keep, send = results[:zs], results[zs:]
        got = [swap(send[k], "col", 1) for k in range(zs)]
        aggregated.append(scatter_terms(keep, got))

    n_parts = len(aggregated[0])
    step = min(STEP, share_rows)
    tile = pl.BlockSpec((step, width), lambda n: (n, 0))
    part_tile = pl.BlockSpec((step, fc), lambda n: (n, 0))
    whole = lambda shape: pl.BlockSpec(shape, lambda n: (0, 0))
    part_shape = jax.ShapeDtypeStruct((share_rows, fc), BF16)
    full_shape = jax.ShapeDtypeStruct((share_rows, width), BF16)
    terms = [term for one in aggregated for term in one]
    dense = pl.pallas_call(
        functools.partial(dense_kernel, n_parts, CHUNKS),
        grid=(share_rows // step,),
        out_shape=[full_shape] * 3 + [jax.ShapeDtypeStruct((8, width), F32), full_shape] + [part_shape] * CHUNKS,
        in_specs=[part_tile] * len(terms) + [whole((width, width)), whole((1, width)), tile],
        out_specs=[tile] * 3 + [whole((8, width)), tile] + [part_tile] * CHUNKS,
        compiler_params=params,
        cost_estimate=pl.CostEstimate(
            flops=4 * share_rows * width * width, bytes_accessed=12 * share_rows * width, transcendentals=share_rows * width
        ),
        name="dense",
    )(*terms, weight, bias.reshape(1, width), cotangent)
    activated, grad_pre, agg, bias_term, mid = dense[:5]
    mids = dense[5:]

    gathered = [gather_pieces(mids[f], zs) for f in range(CHUNKS)]
    own_mirror = swap(mid, "col", 1)

    keep_w, send_w = pl.pallas_call(
        weight_kernel,
        out_shape=[jax.ShapeDtypeStruct((width // 2, width), F32), jax.ShapeDtypeStruct((width // 2 + 8, width), F32)],
        in_specs=[SMEM] + [VMEM] * 3,
        out_specs=[VMEM] * 2,
        scratch_shapes=[pltpu.VMEM((width, width), F32)],
        compiler_params=params,
        cost_estimate=pl.CostEstimate(
            flops=2 * share_rows * width * width, bytes_accessed=6 * width * width, transcendentals=0
        ),
        name="dw",
    )(meta, agg, grad_pre, bias_term)
    keep, extra, packet = keep_w, bias_term, send_w
    levels = [("wc", "row", 1, (1, 0))]
    levels += [(f"wx{bit}", "row", 2 * bit, (1, bit.bit_length())) for bit in bits_below(xs)]
    levels += [("wy", "col", 1, (2, 0))]
    for n, (name, axis, mask, _) in enumerate(levels):
        got = swap(packet, axis, mask)
        if n + 1 < len(levels):
            keep, extra, packet = halve(meta, keep, extra, got, levels[n + 1][3], BF16)
    left = keep.shape[0]
    (both,) = small_call(
        functools.partial(halve_kernel, None), [jax.ShapeDtypeStruct((left + 8, width), BF16)], meta, keep, extra, got
    )
    for bit in reversed(bits_below(zs)):
        both = (both.astype(F32) + swap(both, "col", 2 * bit).astype(F32)).astype(BF16)
    grad_bias = jnp.sum(both[left:].astype(F32), axis=0)
    piece = both[:left]
    for name, axis, mask, place in reversed(levels):
        piece = double(meta, piece, axis, mask, place, F32 if name == "wc" else BF16)
    grad_weight = piece

    for f in range(CHUNKS):
        parts = [mid, own_mirror]
        for k in range(1, zs):
            parts += [gathered[f][k - 1], swap(gathered[f][k - 1], "col", 1)]
        whole_parts = [True, True] + [False] * (cols - 2)
        keep_b, send_b = pl.pallas_call(
            functools.partial(backward_kernel, cols, f, tuple(whole_parts), tile_cols),
            out_shape=[jax.ShapeDtypeStruct((xs, shard_rows, fc), BF16)] * 2,
            in_specs=[SMEM, HBM] + [ANY] * cols,
            out_specs=[VMEM] * 2,
            scratch_shapes=[
                pltpu.VMEM((cols, share_rows, fc), BF16),
                pltpu.VMEM((slots, block, block), BF16),
                pltpu.VMEM((tile_cols, block, fc), F32),
                pltpu.SemaphoreType.DMA((cols,)),
                pltpu.SemaphoreType.DMA((2,)),
            ],
            compiler_params=params,
            cost_estimate=slot_cost,
            name="bwd",
        )(meta, tile_vals, *parts)
        got = swap(send_b, "row", 1)
        near = []
        for k in range(1, xs):
            both = (keep_b[k].astype(F32) + got[k].astype(F32)).astype(BF16)
            near.append(swap(both, "row", 2 * k))
        if f + 1 < CHUNKS:
            early = sum(term.astype(F32) for term in [keep_b[0], got[0]] + near).astype(BF16)
    (grad_in,) = small_call(
        functools.partial(final_kernel, len(near)),
        [jax.ShapeDtypeStruct((shard_rows, width), BF16)],
        meta,
        early,
        keep_b,
        got,
        *near,
    )
    return activated, grad_weight, grad_bias, grad_in


def solution(mesh):
    placed = (
        P(("col", "row"), None),
        P("row", "col", None, None, None),
        P("row", "col", None),
        P("row", "col"),
        P(),
        P(),
        P(("row", "col"), None),
    )

    return jax.shard_map(
        on_device,
        mesh=mesh,
        in_specs=placed,
        out_specs=(P(("row", "col"), None), P(), P(), P(("col", "row"), None)),
        check_vma=False,
    )
```
